512 devices in a mesh: gx: 32 (over y_lo, z), gy: 16 (over y_hi, x, core).
Axes of the slice: x: 4, y: 8 (y_hi: 2, y_lo: 4; y = y_hi * 4 + y_lo), z: 8, core: 2. Of those that a mesh axis runs over, the one named last changes fastest.
Arguments:
- duals: float32 [16, 64, 64, 128], P(None, 'gx', 'gy'), may hold values from -6 to 6
- residual: float32 [16, 64, 64, 128], P(None, 'gx', 'gy')
- direction: float32 [16, 64, 64, 128], P(None, 'gx', 'gy'), may hold values from -6 to 6
- prev_rho: float32 [16], replicated, may hold values from 262144 to 1048576
- dual_schur: float32 [64, 64, 256, 256], P('gx', 'gy'), as said below
- coupling: float32 [64, 64, 8, 256], P('gx', 'gy'), may hold values from -0.75 to 0.75
- coarse_inverse: float32 [32, 384, 384], P('gx'), as said below
- edge_map: int32 [64, 64, 256], P('gx', 'gy'), may hold values from 0 to 255, each once within a row
- corner_slot: int32 [64, 64, 8], P('gx', 'gy'), may hold values from 0 to 384, as said below
- active: int32 [64, 64, 128], P('gx', 'gy'), may hold values 0 or 1
- scaling: float32 [64, 64, 128], P('gx', 'gy'), may hold values from 0.25 to 1
Outputs:
- new_duals: float32 [16, 64, 64, 128], P(None, 'gx', 'gy')
- new_residual: float32 [16, 64, 64, 128], P(None, 'gx', 'gy')
- new_direction: float32 [16, 64, 64, 128], P(None, 'gx', 'gy')
The draws below stay inside these ranges and needn't reach their ends.
Inputs may be any that keep to these rules, and one draw needn't show every extreme that they name: Each subdomain's block of dual_schur and each region's block of coarse_inverse is symmetric positive definite. `coarse_inverse`: each region's block is symmetric positive definite. `corner_slot`: slots number the corner dofs of a region; a corner shared by subdomains of one region has one slot; 384 marks corners on the clamped bottom edge, which have no dof.
All inputs are finite; a program needn't handle non-finite values. No bound on the sum of `active` on one device may be relied on, other than what follows from the above.
Results may differ from the reference program's by a relative error of at most 0.00014.
Values sent between devices are 32-bit elements; how exact they have to be, the bound alone decides.
A program may use at most 64 MiB of HBM per device.

```python
import math
import jax
import jax.numpy as jnp
from jax import lax

NI = 256
NE = 64
NC = 8
K = 16
SX = 2
ITERS = 6
SUBX = 64
SUBY = 64
REGIONS = 32
NCR = 384


def spd_blocks(key, lead, order, scale_lo, scale_hi):
    first, second = jax.random.split(key)
    limit = 0.9 / math.sqrt(order)
    noise = jax.random.uniform(first, lead + (order, order), jnp.float32, -limit, limit)
    sym = 0.5 * (noise + jnp.swapaxes(noise, -1, -2))
    ident = jnp.eye(order, dtype=jnp.float32)
    scales = jnp.exp(jax.random.uniform(second, lead + (order,), jnp.float32, math.log(scale_lo), math.log(scale_hi)))
    return scales[..., :, None] * scales[..., None, :] * (ident + sym)


def draw_dual_schur(key, part):
    return spd_blocks(key, (SUBX, SUBY), NI, 0.4, 1.6)


def draw_coarse_inverse(key, part):
    return spd_blocks(key, (REGIONS,), NCR, 0.45, 0.65)


def draw_residual(key, part):
    cols = jnp.arange(SUBX, dtype=jnp.float32)[None, :, None, None]
    rows = jnp.arange(SUBY, dtype=jnp.float32)[None, None, :, None]
    place = (cols * SUBY + rows) / (SUBX * SUBY)
    shape = (K, SUBX, SUBY, 2 * NE)
    values = jnp.clip(jax.random.normal(key, shape, jnp.float32), -6.0, 6.0)
    return values * jnp.sqrt(1.0 + 2.0 * place)


def draw_corner_slot(key, part):
    cols = jnp.arange(SUBX, dtype=jnp.int32)[:, None, None]
    rows = jnp.arange(SUBY, dtype=jnp.int32)[None, :, None]
    which = jnp.arange(NC, dtype=jnp.int32)[None, None, :]
    corner = which // 2
    dof_id = which % 2
    along = cols % SX + corner % 2
    height = rows + corner // 2
    region = jnp.broadcast_to(cols // SX, (SUBX, SUBY, NC))
    ident = (along * SUBY + (height - 1)) * 2 + dof_id
    ident = jnp.clip(ident, 0, NCR - 1)
    orders = jax.vmap(lambda idx: jax.random.permutation(jax.random.fold_in(key, idx), NCR))(jnp.arange(REGIONS, dtype=jnp.int32))
    slot = orders[region, jnp.broadcast_to(ident, (SUBX, SUBY, NC))].astype(jnp.int32)
    return jnp.where(jnp.broadcast_to(height, (SUBX, SUBY, NC)) == 0, NCR, slot).astype(jnp.int32)


def touch_ends(entries, own_key, smallest, top_value):
    shape = entries.shape
    spot = [jax.random.randint(jax.random.fold_in(own_key, axis), (), 0, shape[axis]) for axis in range(len(shape))]
    entries = entries.at[tuple(spot)].set(smallest)
    longest = shape.index(max(shape))
    spot[longest] = (spot[longest] + 1) % shape[longest]
    return entries.at[tuple(spot)].set(top_value)


def level_of(own_key, extent, pieces, least, largest):
    def one(position, shards_of):
        draws = jax.random.uniform(jax.random.fold_in(jax.random.fold_in(own_key, 6), position), (shards_of,), jnp.float32, least / len(pieces), largest / len(pieces))
        return jnp.repeat(jnp.exp(draws), extent[position] // shards_of).reshape((-1,) + (1,) * (len(extent) - position - 1))

    loudness = one(*pieces[0])
    for cut in pieces[1:]:
        loudness = loudness * one(*cut)
    return loudness


def centred(stream_key, dims, spread, reach, cuts=(), kind=jnp.bfloat16):
    drawn = jax.random.normal(stream_key, dims, jnp.float32) * spread
    if len(cuts) > 0:
        drawn = level_of(stream_key, dims, cuts, -0.22, 0.18) * drawn
    return jnp.clip(drawn, min=-reach, max=reach).astype(kind)


def setup_inputs(seed: int = 0) -> dict:
    key_list = jax.random.split(jax.random.key(seed), 12)
    return {
        "duals": centred(key_list[0], (K, SUBX, SUBY, 2 * NE), 1.0, 6.0, ((1, 32), (2, 16)), jnp.float32),
        "residual": draw_residual(jax.random.fold_in(key_list[11], 71), 0),
        "direction": centred(key_list[2], (K, SUBX, SUBY, 2 * NE), 1.0, 6.0, ((1, 32), (2, 16)), jnp.float32),
        "prev_rho": jnp.clip(jnp.exp(jax.random.uniform(key_list[3], (K,), jnp.float32, math.log(262144.0), math.log(1048576))), 262144.0, 1048576),
        "dual_schur": draw_dual_schur(jax.random.fold_in(key_list[11], 71), 0),
        "coupling": centred(key_list[5], (SUBX, SUBY, NC, NI), (8 * NC) ** -0.5, 0.75, ((0, 32), (1, 16)), jnp.float32),
        "coarse_inverse": draw_coarse_inverse(jax.random.fold_in(key_list[11], 71), 0),
        "edge_map": jax.vmap(lambda own: jax.random.permutation(own, NI))(jax.random.split(key_list[7], SUBX * SUBY)).reshape((SUBX, SUBY, NI)).astype(jnp.int32),
        "corner_slot": draw_corner_slot(jax.random.fold_in(key_list[11], 71), 0),
        "active": touch_ends((jax.random.randint(key_list[9], (SUBX, SUBY, 2 * NE), 0, 8) < 7).astype(jnp.int32), jax.random.fold_in(key_list[9], 1), 0, 1),
        "scaling": jnp.clip(jnp.exp(math.log(1.0) - 1.3862944 * jax.random.uniform(key_list[10], (SUBX, SUBY, 2 * NE), jnp.float32) ** level_of(key_list[10], (SUBX, SUBY, 2 * NE), ((0, 32), (1, 16)), -0.2, 0.2)), 0.25, 1.0),
    }


def make_keep(active):
    east = (jnp.arange(SUBX) < SUBX - 1)[:, None, None]
    north = (jnp.arange(SUBY) < SUBY - 1)[None, :, None]
    east = jnp.broadcast_to(east, (SUBX, SUBY, NE))
    north = jnp.broadcast_to(north, (SUBX, SUBY, NE))
    return active.astype(jnp.float32) * jnp.concatenate([east, north], -1).astype(jnp.float32)


def apply_dual(field, keep, dual_schur, coupling, coarse_inverse, edge_map, inverse, onehot):
    high = lax.Precision.HIGHEST
    part_e = field[..., :NE]
    part_n = field[..., NE:]
    west = -jnp.pad(part_e, ((0, 0), (1, 0), (0, 0), (0, 0)))[:, :-1]
    south = -jnp.pad(part_n, ((0, 0), (0, 0), (1, 0), (0, 0)))[:, :, :-1]
    edge_vec = jnp.concatenate([west, part_e, south, part_n], -1)
    local = jnp.take_along_axis(edge_vec, edge_map[None], -1)
    work = jnp.einsum('xyij,kxyj->kxyi', dual_schur, local, precision=high)
    corner_val = jnp.einsum('xycj,kxyj->kxyc', coupling, local, precision=high)
    grouped = corner_val.reshape(K, REGIONS, SX, SUBY, NC)
    table = onehot.reshape(REGIONS, SX, SUBY, NC, NCR)
    total = jnp.einsum('krayc,raycn->krn', grouped, table, precision=high)
    solved = jnp.einsum('rnm,krm->krn', coarse_inverse, total, precision=high)
    back = jnp.einsum('raycn,krn->krayc', table, solved, precision=high).reshape(K, SUBX, SUBY, NC)
    work = work + jnp.einsum('xycj,kxyc->kxyj', coupling, back, precision=high)
    work_edge = jnp.take_along_axis(work, inverse[None], -1)
    west_w = work_edge[..., :NE]
    east_w = work_edge[..., NE:2 * NE]
    south_w = work_edge[..., 2 * NE:3 * NE]
    north_w = work_edge[..., 3 * NE:]
    from_east = jnp.pad(west_w, ((0, 0), (0, 1), (0, 0), (0, 0)))[:, 1:]
    from_north = jnp.pad(south_w, ((0, 0), (0, 0), (0, 1), (0, 0)))[:, :, 1:]
    return jnp.concatenate([east_w - from_east, north_w - from_north], -1) * keep


def reference(duals, residual, direction, prev_rho, dual_schur, coupling, coarse_inverse, edge_map, corner_slot, active, scaling):
    keep = make_keep(active)
    inverse = jnp.argsort(edge_map, axis=-1).astype(jnp.int32)
    onehot = (corner_slot[..., None] == jnp.arange(NCR, dtype=jnp.int32)).astype(jnp.float32)
    lam = duals
    res = residual
    pprev = keep * direction
    rho_old = prev_rho
    for step in range(ITERS):
        zvec = keep * scaling * res
        rho = jnp.sum(res * zvec, axis=(1, 2, 3))
        beta = rho / rho_old
        pvec = zvec + beta[:, None, None, None] * pprev
        qvec = apply_dual(pvec, keep, dual_schur, coupling, coarse_inverse, edge_map, inverse, onehot)
        alpha = rho / jnp.sum(pvec * qvec, axis=(1, 2, 3))
        lam = lam + alpha[:, None, None, None] * pvec
        res = res - alpha[:, None, None, None] * qvec
        rho_old = rho
        pprev = pvec
    return lam, res, pprev
```

```python
import functools

import jax
import jax.numpy as jnp
from jax import lax
from jax.experimental import pallas as pl
from jax.experimental.pallas import tpu as pltpu
from jax.sharding import PartitionSpec as P

MESH = pl.DeviceIdType.MESH
NT = (((1,), (1,)), ((), ()))
F32 = jnp.float32
BF16 = jnp.bfloat16


def dot(a, b):
    return jnp.dot(a, b, preferred_element_type=F32)


def dot_nt(a, b):
    return lax.dot_general(a, b, NT, preferred_element_type=F32)


def split(v):
    hi = v.astype(BF16)
    return hi, (v - hi.astype(F32)).astype(BF16)


def iota(shape, dim):
    return lax.broadcasted_iota(jnp.int32, shape, dim)


def remote(src, dst, send, recv, dev):
    return pltpu.make_async_remote_copy(
        src_ref=src, dst_ref=dst, send_sem=send, recv_sem=recv, device_id=dev, device_id_type=MESH
    )


class Group:
    def __init__(self, n, me, dev, src, dst, send, recv):
        self.n, self.me, self.dev, self.src, self.dst, self.send_sem, self.recv_sem = n, me, dev, src, dst, send, recv

    def each(self, fn):
        def body(j, c):
            fn(j)
            return c

        lax.fori_loop(1, self.n, body, 0, unroll=True)

    def copy_to(self, j):
        peer = lax.rem(self.me + j, self.n)
        return remote(self.src, self.dst.at[self.me], self.send_sem.at[j], self.recv_sem.at[self.me], self.dev(peer))

    def copy_from(self, j):
        peer = lax.rem(self.me + j, self.n)
        return remote(self.src, self.dst.at[peer], self.send_sem.at[j], self.recv_sem.at[peer], self.dev(peer))

    def start(self, value):
        self.src[...] = value
        self.dst[self.me] = value
        self.each(lambda j: self.copy_to(j).start())

    def wait(self):
        self.each(lambda j: self.copy_from(j).wait_recv())

    def finish(self):
        self.each(lambda j: self.copy_to(j).wait_send())


def kernel(
    gxn, gyn, zn, iters,
    duals, residual, direction, misc, schur, coupling, ainv, emap, active, scaling,
    out_l, out_r, out_p,
    s_hi, s_lo, g_hi, g_lo, m_hi, m_lo, lhs,
    lam, res, pv, qv, wv, tv, xv, keep, dv, wk, wn,
    h_w, h_s, r_e, r_n, g1, ct, d1, d2, d3, c1, c2, c3, sl, slsrc, sc,
    hsend, hrecv, gsend, grecv, d1s, d1r, d2s, d2r, d3s, d3r, sls, slr,
):
    gx = lax.axis_index("gx")
    gy = lax.axis_index("gy")
    yn = gxn // zn
    zpos, ypos = lax.rem(gx, zn), gx // zn
    has_w, has_e = gx > 0, gx < gxn - 1
    has_s, has_n = gy > 0, gy < gyn - 1
    by_y = lambda i: (gx, i)
    by_z = lambda i: (ypos * zn + i, gy)
    by_o = lambda i: (i * zn + zpos, gy)

    for ref in (h_w, h_s, r_e, r_n):
        ref[...] = jnp.zeros_like(ref)

    barrier = pltpu.get_barrier_semaphore()

    def greet(n, me, dev):
        def body(j, c):
            pl.semaphore_signal(barrier, inc=1, device_id=dev(lax.rem(me + j, n)), device_id_type=MESH)
            return c

        lax.fori_loop(1, n, body, 0, unroll=True)

    greet(gyn, gy, by_y)
    greet(zn, zpos, by_z)
    greet(yn, ypos, by_o)

    @pl.when(has_e)
    def _():
        pl.semaphore_signal(barrier, inc=1, device_id=(gx + 1, gy), device_id_type=MESH)

    @pl.when(has_w)
    def _():
        pl.semaphore_signal(barrier, inc=1, device_id=(gx - 1, gy), device_id_type=MESH)

    lane = iota((16, 128), 1)
    row = iota((16, 128), 0)
    low = lane < 64
    low8 = iota((8, 128), 1) < 64

    for a in range(2):
        for b in range(4):
            s = a * 4 + b
            lam[s] = duals[:, a, b, :]
            res[s] = residual[:, a, b, :]
            kp = jnp.broadcast_to(active[a, b : b + 1, :].astype(F32), (16, 128))
            if a == 1:
                kp = jnp.where(jnp.logical_or(has_e, lane >= 64), kp, 0.0)
            if b == 3:
                kp = jnp.where(jnp.logical_or(has_n, lane < 64), kp, 0.0)
            keep[s] = kp
            dv[s] = kp * jnp.broadcast_to(scaling[a, b : b + 1, :], (16, 128))
            pv[s] = kp * direction[:, a, b, :]

    def dots(pairs):
        acc = jnp.zeros((16, 128), F32)
        for d, prod in enumerate(pairs):
            col = jnp.sum(jnp.sum(prod, axis=0), axis=1, keepdims=True)
            acc = jnp.where(lane == row + 16 * d, jnp.broadcast_to(col, (16, 128)), acc)
        return jnp.sum(acc, axis=0, keepdims=True)

    def column(line, d):
        picked = jnp.where(lane == row + 16 * d, jnp.broadcast_to(line, (16, 128)), 0.0)
        return jnp.broadcast_to(jnp.sum(picked, axis=1, keepdims=True), (16, 128))

    def stages(par):
        return (
            Group(gyn, gy, by_y, c1, d1.at[par], d1s, d1r.at[par]),
            Group(zn, zpos, by_z, c2, d2.at[par], d2s, d2r.at[par]),
            Group(yn, ypos, by_o, c3, d3.at[par], d3s, d3r.at[par]),
        )

    def total(group):
        group.wait()
        return jnp.sum(group.dst[...], axis=0)

    slots = Group(gyn, gy, by_y, slsrc, sl, sls, slr)
    first = stages(0)
    rho_line = dots([res[...] * (dv[...] * res[...])])

    pl.semaphore_wait(
        barrier, (gyn - 1) + (zn - 1) + (yn - 1) + has_e.astype(jnp.int32) + has_w.astype(jnp.int32)
    )
    first[0].start(rho_line)
    slots.start(misc[0])

    e = iota((256, 256), 0)
    orig = jnp.where(e < 64, e + 64, jnp.where(e < 128, e + 128, jnp.where(e < 192, e - 128, e - 64)))
    sign = jnp.where(e < 128, 1.0, -1.0)
    grow = iota((128, 256), 0)
    for a in range(2):
        for b in range(4):
            s = a * 4 + b
            em = jnp.broadcast_to(emap[a, b : b + 1, :], (256, 256))
            pt = jnp.where(em == orig, sign, 0.0).astype(BF16)
            sh, slo = split(schur[s])
            s_hi[s] = dot(pt, dot_nt(sh, pt).astype(BF16)).astype(BF16)
            s_lo[s] = dot(pt, dot_nt(slo, pt).astype(BF16)).astype(BF16)
            ch, cl = split(coupling[s])
            here = (grow % 64) // 8 == s
            for part, ref in ((ch, g_hi), (cl, g_lo)):
                turned = dot_nt(part, pt)
                ref[s] = jnp.where(here, jnp.concatenate([turned] * 16, axis=0), 0.0).astype(BF16)
        if a == 0:
            first[1].start(total(first[0]))
    first[2].start(total(first[1]))

    width = ainv.shape[0]
    slots.wait()
    own = jnp.transpose(jnp.broadcast_to(misc[0], (128, 128)))
    own_hot = jnp.where(
        jnp.concatenate([own] * (width // 128), axis=1) == iota((128, width), 1).astype(F32), 1.0, 0.0
    ).astype(BF16)
    ah, al = split(ainv[...])
    yh, yl = dot(own_hot, ah).astype(BF16), dot(own_hot, al).astype(BF16)
    tall = iota((width, 128), 0).astype(F32)
    for pair in range(gyn // 2):
        both = jnp.where(low8[:1], sl[2 * pair], pltpu.roll(sl[2 * pair + 1], 64, 1))
        hot = jnp.where(tall == jnp.broadcast_to(both, (width, 128)), 1.0, 0.0).astype(BF16)
        cols = slice(pair * 128, pair * 128 + 128)
        m_hi[:, cols] = dot(yh, hot).astype(BF16)
        m_lo[:, cols] = dot(yl, hot).astype(BF16)

    line = total(first[2])
    rho = column(line, 0)
    beta = rho / column(misc[1], 0)
    pv[...] = dv[...] * res[...] + beta * pv[...]
    xv[...] = pv[...].reshape(2, 4, 16, 128)
    sc[0] = rho
    sc[1] = rho
    for group in first:
        group.finish()
    slots.finish()

    def halo(par):
        return (
            remote(xv.at[1], h_w.at[par], hsend.at[0], hrecv.at[par, 0], (gx + 1, gy)),
            remote(xv.at[:, 3], h_s.at[par], hsend.at[1], hrecv.at[par, 1], (gx, gy + 1)),
            remote(wn.at[0], r_e.at[par], hsend.at[2], hrecv.at[par, 2], (gx - 1, gy)),
            remote(wn.at[:, 0], r_n.at[par], hsend.at[3], hrecv.at[par, 3], (gx, gy - 1)),
        )

    sends = (has_e, has_n, has_w, has_s)
    receives = (has_w, has_s, has_e, has_n)

    def each_of(copies, which, go, verb):
        for i in which:
            pl.when(go[i])(lambda i=i: getattr(copies[i], verb)())

    def fold(v):
        return v[:16] + v[16:]

    def apply(par, line):
        copies = halo(par)
        reduce_y, reduce_z, reduce_o = stages(par)
        coarse = Group(gyn, gy, by_y, ct, g1.at[par], gsend, grecv.at[par])
        each_of(copies, (0, 1), sends, "start")
        reduce_y.start(line)
        each_of(copies, (0, 1), receives, "wait_recv")
        v2 = jnp.zeros((16, 128), F32)
        for a in range(2):
            for b in range(4):
                s = a * 4 + b
                west = h_w[par, b] if a == 0 else xv[0, b]
                south = h_s[par, a] if b == 0 else xv[a, b - 1]
                hi, lo = split(jnp.concatenate([xv[a, b], jnp.where(low, west, south)], axis=1))
                lhs[s, :16] = hi
                lhs[s, 16:] = lo
                v2 = v2 + fold(dot_nt(jnp.concatenate([hi, lo], axis=0), g_hi[s])) + dot_nt(hi, g_lo[s])
        coarse.start(jnp.where(low8, v2[:8], v2[8:]))
        reduce_z.start(total(reduce_y))
        for s in range(8):
            wk[s] = fold(dot(lhs[s], s_hi[s])) + dot(lhs[s, :16], s_lo[s])
        coarse.wait()
        pieces = []
        for pair in range(gyn // 2):
            one, two = g1[par, 2 * pair], g1[par, 2 * pair + 1]
            top = jnp.where(low8, one, pltpu.roll(two, 64, 1))
            bottom = jnp.where(low8, pltpu.roll(one, 64, 1), two)
            pieces.append(jnp.concatenate([top, bottom], axis=0))
        hi, lo = split(jnp.concatenate(pieces, axis=1))
        back = fold(dot_nt(jnp.concatenate([hi, lo], axis=0), m_hi[...])) + dot_nt(hi, m_lo[...])
        bhi, blo = split(back)
        bhl = jnp.concatenate([bhi, blo], axis=0)
        for s in range(8):
            full = wk[s] + fold(dot(bhl, g_hi[s])) + dot(bhi, g_lo[s])
            wk[s] = full
            wn[s // 4, s % 4] = full[:, 128:]
        each_of(copies, (2, 3), sends, "start")
        reduce_o.start(total(reduce_z))
        summed = total(reduce_o)
        each_of(copies, (2, 3), receives, "wait_recv")
        result = []
        for a in range(2):
            for b in range(4):
                east = r_e[par, b] if a == 1 else wn[1, b]
                north = r_n[par, a] if b == 3 else wn[a, b + 1]
                result.append(wk[a * 4 + b, :, :128] + jnp.where(low, east, north))
        each_of(copies, (0, 1, 2, 3), sends, "wait_send")
        for group in (reduce_y, reduce_z, reduce_o, coarse):
            group.finish()
        return jnp.stack(result) * keep[...], summed

    def residual_dots():
        z = dv[...] * res[...]
        return dots([res[...] * z, z * wv[...], z * qv[...]])

    def step_of(line):
        rho = column(line, 0)
        beta = rho / sc[0]
        pq = column(line, 1) + beta * (2.0 * column(line, 2) + beta * sc[1])
        alpha = rho / pq
        sc[0] = rho
        sc[1] = pq
        return beta, alpha, dv[...] * res[...] + beta * pv[...]

    def round_body(i, line):
        got, summed = apply(lax.rem(i + 1, 2), line)
        nxt = c1

        @pl.when(i == 0)
        def _():
            qv[...] = got
            xv[...] = (dv[...] * got).reshape(2, 4, 16, 128)
            nxt[...] = dots([pv[...] * got])

        @pl.when(i == 1)
        def _():
            tv[...] = got
            pq = column(summed, 0)
            alpha = sc[0] / pq
            sc[1] = pq
            lam[...] += alpha * pv[...]
            new = res[...] - alpha * qv[...]
            res[...] = new
            xv[...] = (dv[...] * new).reshape(2, 4, 16, 128)

        @pl.when(i == 2)
        def _():
            wv[...] = got
            xv[...] = (dv[...] * got).reshape(2, 4, 16, 128)
            nxt[...] = residual_dots()

        @pl.when(i >= 3)
        def _():
            beta, alpha, p = step_of(summed)
            pv[...] = p
            q = wv[...] + beta * qv[...]
            t = got + beta * tv[...]
            qv[...] = q
            tv[...] = t
            lam[...] += alpha * p
            res[...] -= alpha * q
            w = wv[...] - alpha * t
            wv[...] = w
            xv[...] = (dv[...] * w).reshape(2, 4, 16, 128)
            nxt[...] = residual_dots()

        return nxt[...]

    rounds = iters + 1
    line = lax.fori_loop(0, rounds, round_body, rho_line)

    last = stages((rounds + 1) % 2)
    last[0].start(line)
    last[1].start(total(last[0]))
    last[2].start(total(last[1]))
    beta, alpha, p = step_of(total(last[2]))
    new_l = lam[...] + alpha * p
    new_r = res[...] - alpha * (wv[...] + beta * qv[...])
    for a in range(2):
        for b in range(4):
            s = a * 4 + b
            out_l[:, a, b, :] = new_l[s]
            out_r[:, a, b, :] = new_r[s]
            out_p[:, a, b, :] = p[s]
    for group in last:
        group.finish()


def shards(gxn, gyn, zn, duals, residual, direction, prev_rho, schur, coupling, ainv, emap, slot, active, scaling):
    misc = jnp.stack([
        jnp.pad(slot.reshape(1, 64).astype(F32), ((0, 0), (0, 64)), constant_values=float(ainv.shape[-1])),
        jnp.pad(prev_rho.reshape(1, 16), ((0, 0), (0, 112))),
    ])
    yn = gxn // zn
    vmem = pl.BlockSpec(memory_space=pltpu.VMEM)
    field = jax.ShapeDtypeStruct(duals.shape, F32)
    tiles = lambda *lead: pltpu.VMEM(lead + (16, 128), F32)
    line = lambda *lead: pltpu.VMEM(lead + (1, 128), F32)
    dma = lambda *shape: pltpu.SemaphoreType.DMA(shape)
    return pl.pallas_call(
        functools.partial(kernel, gxn, gyn, zn, 6),
        out_shape=(field, field, field),
        in_specs=[vmem] * 10,
        out_specs=(vmem, vmem, vmem),
        scratch_shapes=[
            pltpu.VMEM((8, 256, 256), BF16), pltpu.VMEM((8, 256, 256), BF16),
            pltpu.VMEM((8, 128, 256), BF16), pltpu.VMEM((8, 128, 256), BF16),
            pltpu.VMEM((128, 64 * gyn), BF16), pltpu.VMEM((128, 64 * gyn), BF16),
            pltpu.VMEM((8, 32, 256), BF16),
            tiles(8), tiles(8), tiles(8), tiles(8), tiles(8), tiles(8), tiles(2, 4), tiles(8), tiles(8),
            pltpu.VMEM((8, 16, 256), F32), tiles(2, 4),
            tiles(2, 4), tiles(2, 2), tiles(2, 4), tiles(2, 2),
            pltpu.VMEM((2, gyn, 8, 128), F32), pltpu.VMEM((8, 128), F32),
            line(2, gyn), line(2, zn), line(2, yn), line(), line(), line(),
            line(gyn), line(), tiles(2),
            dma(4), dma(2, 4), dma(gyn), dma(2, gyn),
            dma(gyn), dma(2, gyn), dma(zn), dma(2, zn), dma(yn), dma(2, yn), dma(gyn), dma(gyn),
        ],
        compiler_params=pltpu.CompilerParams(collective_id=0, has_side_effects=True),
    )(duals, residual, direction, misc, schur.reshape(8, 256, 256), coupling.reshape(8, 8, 256), ainv[0], emap, active, scaling)


def solution(mesh):
    gxn, gyn = mesh.shape["gx"], mesh.shape["gy"]
    zn = 8 if gxn % 8 == 0 else 2
    grid = P(None, "gx", "gy", None)
    cells = P("gx", "gy", None)
    return jax.shard_map(
        functools.partial(shards, gxn, gyn, zn),
        mesh=mesh,
        in_specs=(
            grid, grid, grid, P(), P("gx", "gy", None, None), P("gx", "gy", None, None), P("gx", None, None),
            cells, cells, cells, cells,
        ),
        out_specs=(grid, grid, grid),
        check_vma=False,
    )
```

```python
import functools

import jax
import jax.numpy as jnp
from jax import lax
from jax.experimental import pallas as pl
from jax.experimental.pallas import tpu as pltpu
from jax.sharding import PartitionSpec as P

MESH = pl.DeviceIdType.MESH
NT = (((1,), (1,)), ((), ()))
F32 = jnp.float32
BF16 = jnp.bfloat16


def dot(a, b):
    return jnp.dot(a, b, preferred_element_type=F32)


def dot_nt(a, b):
    return lax.dot_general(a, b, NT, preferred_element_type=F32)


def split(v):
    hi = v.astype(BF16)
    return hi, (v - hi.astype(F32)).astype(BF16)


def iota(shape, dim):
    return lax.broadcasted_iota(jnp.int32, shape, dim)


def remote(src, dst, send, recv, dev):
    return pltpu.make_async_remote_copy(
        src_ref=src, dst_ref=dst, send_sem=send, recv_sem=recv, device_id=dev, device_id_type=MESH
    )


class Group:
    def __init__(self, n, me, dev, src, dst, send, recv):
        self.n, self.me, self.dev, self.src, self.dst, self.send_sem, self.recv_sem = n, me, dev, src, dst, send, recv

    def each(self, fn):
        def body(j, c):
            fn(j)
            return c

        lax.fori_loop(1, self.n, body, 0, unroll=True)

    def copy_to(self, j):
        peer = lax.rem(self.me + j, self.n)
        return remote(self.src, self.dst.at[self.me], self.send_sem.at[j], self.recv_sem.at[self.me], self.dev(peer))

    def copy_from(self, j):
        peer = lax.rem(self.me + j, self.n)
        return remote(self.src, self.dst.at[peer], self.send_sem.at[j], self.recv_sem.at[peer], self.dev(peer))

    def start(self, value):
        self.src[...] = value
        self.dst[self.me] = value
        self.each(lambda j: self.copy_to(j).start())

    def wait(self):
        self.each(lambda j: self.copy_from(j).wait_recv())

    def finish(self):
        self.each(lambda j: self.copy_to(j).wait_send())


def kernel(
    gxn, gyn, zn, yhn, iters,
    duals, residual, direction, prev_rho, schur, coupling, ainv, emap, slot, active, scaling,
    out_l, out_r, out_p,
    s_hi, s_lo, g_hi, g_lo, m_hi, m_lo, lhs,
    lam, res, pv, qv, wv, tv, xv, keep, dv, wk, wn,
    h_w, h_s, r_e, h_n, h_nw, g1, ct, d1, d2, d3, c1, c2, c3, sl, slsrc, sc,
    n_src, n_dst, k_src, k_dst, f_src, f_dst, n_hi, n_lo, gn_hi, gn_lo, small,
    hsend, hrecv, gsend, grecv, d1s, d1r, d2s, d2r, d3s, d3r, sls, slr, nsend, nrecv,
):
    gx = lax.axis_index("gx")
    gy = lax.axis_index("gy")
    yln, xcn = gxn // zn, gyn // yhn
    yn = yln * yhn
    zpos, xcpos = lax.rem(gx, zn), lax.rem(gy, xcn)
    ypos = (gy // xcn) * yln + gx // zn
    has_w, has_e = gx > 0, gx < gxn - 1
    has_s, has_n = gy > 0, gy < gyn - 1
    has_se = jnp.logical_and(has_e, has_s)
    has_nw = jnp.logical_and(has_w, has_n)
    by_y = lambda i: (gx, i)
    by_z = lambda i: ((gx // zn) * zn + i, gy)
    by_x = lambda i: (gx, (gy // xcn) * xcn + i)
    by_o = lambda i: (lax.rem(i, yln) * zn + zpos, (i // yln) * xcn + xcpos)

    for ref in (h_w, h_s, r_e, h_n, h_nw, n_dst, k_dst, small):
        ref[...] = jnp.zeros_like(ref)
    none = float(ainv.shape[0])
    f_dst[...] = jnp.full(f_dst.shape, none, F32)

    barrier = pltpu.get_barrier_semaphore()

    def greet(n, me, dev):
        def body(j, c):
            pl.semaphore_signal(barrier, inc=1, device_id=dev(lax.rem(me + j, n)), device_id_type=MESH)
            return c

        lax.fori_loop(1, n, body, 0, unroll=True)

    greet(gyn, gy, by_y)
    greet(zn, zpos, by_z)
    greet(yn, ypos, by_o)

    @pl.when(has_e)
    def _():
        pl.semaphore_signal(barrier, inc=1, device_id=(gx + 1, gy), device_id_type=MESH)

    @pl.when(has_w)
    def _():
        pl.semaphore_signal(barrier, inc=1, device_id=(gx - 1, gy), device_id_type=MESH)

    @pl.when(has_se)
    def _():
        pl.semaphore_signal(barrier, inc=1, device_id=(gx + 1, gy - 1), device_id_type=MESH)

    @pl.when(has_nw)
    def _():
        pl.semaphore_signal(barrier, inc=1, device_id=(gx - 1, gy + 1), device_id_type=MESH)

    lane = iota((16, 128), 1)
    row = iota((16, 128), 0)
    low = lane < 64
    low8 = iota((8, 128), 1) < 64

    for a in range(2):
        for b in range(4):
            s = a * 4 + b
            lam[s] = duals[:, a, b, :]
            res[s] = residual[:, a, b, :]
            kp = jnp.broadcast_to(active[a, b : b + 1, :].astype(F32), (16, 128))
            if a == 1:
                kp = jnp.where(jnp.logical_or(has_e, lane >= 64), kp, 0.0)
            if b == 3:
                kp = jnp.where(jnp.logical_or(has_n, lane < 64), kp, 0.0)
            keep[s] = kp
            dv[s] = kp * jnp.broadcast_to(scaling[a, b : b + 1, :], (16, 128))
            pv[s] = kp * direction[:, a, b, :]
            xv[a, b, :16] = dv[s] * res[s]
            xv[a, b, 16:] = pv[s]

    def dots(pairs):
        acc = jnp.zeros((16, 128), F32)
        for d, prod in enumerate(pairs):
            col = jnp.sum(jnp.sum(prod, axis=0), axis=1, keepdims=True)
            acc = jnp.where(lane == row + 16 * d, jnp.broadcast_to(col, (16, 128)), acc)
        return jnp.sum(acc, axis=0, keepdims=True)

    def column(line, d):
        picked = jnp.where(lane == row + 16 * d, jnp.broadcast_to(line, (16, 128)), 0.0)
        return jnp.broadcast_to(jnp.sum(picked, axis=1, keepdims=True), (16, 128))

    def stages(par):
        return (
            Group(xcn, xcpos, by_x, c1, d1.at[par], d1s, d1r.at[par]),
            Group(yn, ypos, by_o, c2, d2.at[par], d2s, d2r.at[par]),
            Group(zn, zpos, by_z, c3, d3.at[par], d3s, d3r.at[par]),
        )

    def total(group):
        group.wait()
        return jnp.sum(group.dst[...], axis=0)

    for a in range(2):
        for b in range(4):
            small[a * 4 + b : a * 4 + b + 1, :8] = slot[a, b : b + 1, :].astype(F32)
    small[8:9, :16] = prev_rho[...]
    spread = jnp.where(iota((128, 128), 0) == iota((128, 128), 1) % 8, 1.0, 0.0)
    each = jnp.dot(small[:8], spread, precision=lax.Precision.HIGHEST, preferred_element_type=F32)
    lane8 = iota((8, 128), 1)
    own_row = jnp.sum(jnp.where(lane8 // 8 == iota((8, 128), 0), each, 0.0), axis=0, keepdims=True)
    own_row = jnp.where(lane8[:1] < 64, own_row, none)
    f_src[...] = own_row

    slots = Group(gyn, gy, by_y, slsrc, sl, sls, slr)

    e = iota((256, 256), 0)
    orig = jnp.where(e < 64, e + 64, jnp.where(e < 128, e + 128, jnp.where(e < 192, e - 128, e - 64)))
    sign = jnp.where(e < 128, 1.0, -1.0)
    def turn(s):
        em = jnp.broadcast_to(emap[s // 4, s % 4 : s % 4 + 1, :], (256, 256))
        pt = jnp.where(em == orig, sign, 0.0).astype(BF16)
        sh, slo = split(schur[s])
        parts = dot(pt, dot_nt(sh, pt).astype(BF16)), dot(pt, dot_nt(slo, pt).astype(BF16))
        s_hi[s] = parts[0].astype(BF16)
        s_lo[s] = parts[1].astype(BF16)
        ch, cl = split(coupling[s])
        g_hi[s, :8] = dot_nt(ch, pt).astype(BF16)
        g_lo[s, :8] = dot_nt(cl, pt).astype(BF16)
        return parts

    def packed(first_half, second_half):
        return jnp.where(iota(first_half.shape, 1) < 64, pltpu.roll(first_half, 64, 1), second_half)

    zero, four = turn(0), turn(4)
    n_src[...] = packed((zero[0] + zero[1])[:, 128:], (four[0] + four[1])[:, 128:])
    corner = [(g_hi[s, :8].astype(F32) + g_lo[s, :8].astype(F32))[:, 128:] for s in (0, 4)]
    k_src[...] = packed(corner[0], corner[1])

    pl.semaphore_wait(
        barrier,
        (gyn - 1) + (zn - 1) + (yn - 1)
        + has_e.astype(jnp.int32) + has_w.astype(jnp.int32)
        + has_se.astype(jnp.int32) + has_nw.astype(jnp.int32),
    )
    south = (gx, gy - 1)
    early = (
        remote(f_src, f_dst, nsend.at[0], nrecv.at[0], south),
        remote(k_src, k_dst, nsend.at[1], nrecv.at[1], south),
        remote(n_src, n_dst, nsend.at[2], nrecv.at[2], south),
    )
    pl.when(has_s)(lambda: early[0].start())
    pl.when(has_s)(lambda: early[1].start())

    line_id = iota((1, 128), 1)
    sub, lan = iota((128, 128), 0), iota((128, 128), 1)
    square = lambda v: jnp.broadcast_to(v, (128, 128))
    width = ainv.shape[0]
    held = {}

    def number_corners():
        pl.when(has_s)(lambda: early[2].start())
        turn(1)
        turn(2)
        pl.when(has_n)(lambda: early[0].wait_recv())
        above = f_dst[...]
        ext = jnp.where(line_id < 64, own_row, jnp.where(
            line_id < 72, pltpu.roll(above, 64, 1), jnp.where(line_id < 80, pltpu.roll(above, 40, 1), none)
        ))
        ext_r = square(ext)
        ext_c = jnp.transpose(ext_r)
        seen = jnp.sum(jnp.where(jnp.logical_and(ext_c == ext_r, sub < lan), 1.0, 0.0), axis=0, keepdims=True)
        lead = jnp.where(jnp.logical_and(seen == 0.0, ext < none), 1.0, 0.0)
        lead_c = jnp.transpose(square(lead))
        rank = jnp.sum(jnp.where(ext_c < ext_r, lead_c, 0.0), axis=0, keepdims=True)
        rank_c = jnp.transpose(square(rank))
        chosen = jnp.sum(jnp.where(rank_c == lan.astype(F32), lead_c * (ext_c - none), 0.0), axis=0, keepdims=True)
        slots.start(chosen + none)
        pick = jnp.where(jnp.logical_and(square(rank) == (sub % 64).astype(F32), ext_r < none), 1.0, 0.0)
        for s in (3, 5, 6, 7):
            turn(s)
        for s in range(8):
            mine = jnp.where(lan // 8 == s, pick, 0.0).astype(BF16)
            for ref in (g_hi, g_lo):
                rows = jnp.concatenate([ref[s, :8].astype(F32)] * 16, axis=0).astype(BF16)
                ref[s] = dot(mine, rows).astype(BF16)
        pl.when(has_n)(lambda: early[1].wait_recv())
        upper = jnp.concatenate([k_dst[...]] * 16, axis=0)
        halves = []
        for a in range(2):
            mine = jnp.where(lan // 8 == 8 + a, pick, 0.0).astype(BF16)
            halves.append([dot(mine, part) for part in split(upper)])
        gn_hi[...] = jnp.where(lan < 64, halves[0][0], halves[1][0]).astype(BF16)
        gn_lo[...] = jnp.where(lan < 64, halves[0][1], halves[1][1]).astype(BF16)
        corners = jnp.where(
            jnp.concatenate([ext_c] * (width // 128), axis=1) == iota((128, width), 1).astype(F32), 1.0, 0.0
        )
        held["hot"] = jnp.where(jnp.logical_and(sub < 64, square(lead) > 0.0), pick, 0.0), corners

    def own_inverse():
        own_hot = dot(held["hot"][0].astype(BF16), held["hot"][1].astype(BF16)).astype(BF16)
        ah, al = split(ainv[...])
        held["rows"] = dot(own_hot, ah).astype(BF16), dot(own_hot, al).astype(BF16)

    def upper_block():
        pl.when(has_n)(lambda: early[2].wait_recv())
        nh, nl = split(n_dst[...])
        n_hi[...] = nh
        n_lo[...] = nl

    def region_inverse():
        tall = iota((width, 128), 0).astype(F32)
        slots.wait()
        yh, yl = held["rows"]
        for pair in range(gyn // 2):
            both = jnp.where(low8[:1], sl[2 * pair], pltpu.roll(sl[2 * pair + 1], 64, 1))
            hot = jnp.where(tall == jnp.broadcast_to(both, (width, 128)), 1.0, 0.0).astype(BF16)
            cols = slice(pair * 128, pair * 128 + 128)
            m_hi[:, cols] = dot(yh, hot).astype(BF16)
            m_lo[:, cols] = dot(yl, hot).astype(BF16)

    def halo(par, rows):
        r = pl.ds(0, rows)
        return (
            remote(xv.at[1, :, r], h_w.at[par, :, r], hsend.at[0], hrecv.at[par, 0], (gx + 1, gy)),
            remote(xv.at[:, 3, r], h_s.at[par, :, r], hsend.at[1], hrecv.at[par, 1], (gx, gy + 1)),
            remote(xv.at[:, 0, r], h_n.at[par, :, r], hsend.at[2], hrecv.at[par, 2], (gx, gy - 1)),
            remote(xv.at[1, 0, r], h_nw.at[par, r], hsend.at[3], hrecv.at[par, 3], (gx + 1, gy - 1)),
            remote(wn.at[:, r], r_e.at[par, :, r], hsend.at[4], hrecv.at[par, 4], (gx - 1, gy)),
        )

    sends = (has_e, has_n, has_s, has_se, has_w)
    receives = (has_w, has_s, has_n, has_nw, has_e)

    def each_of(copies, which, go, verb):
        for i in which:
            pl.when(go[i])(lambda i=i: getattr(copies[i], verb)())

    def fold(v):
        return v[: v.shape[0] // 2] + v[v.shape[0] // 2 :]

    def three(both, hi, high, low_part, product):
        return fold(product(both, high)) + product(hi, low_part)

    def apply(par, fields, line, hooks):
        nothing = lambda: None
        rows = 16 * fields
        low = iota((rows, 128), 1) < 64
        copies = halo(par, rows)
        coarse = Group(
            gyn, gy, by_y, ct.at[: 8 * fields], g1.at[par, :, : 8 * fields], gsend, grecv.at[par]
        )
        groups = stages(par) if line is not None else ()
        each_of(copies, (0, 1, 2, 3), sends, "start")
        if groups:
            groups[0].start(line)
        hooks.get("corners", nothing)()
        each_of(copies, (0,), receives, "wait_recv")
        if groups:
            groups[1].start(total(groups[0]))
        hi, lo = split(packed(xv[0, 3, :rows], xv[1, 3, :rows]))
        v2 = three(jnp.concatenate([hi, lo], axis=0), hi, gn_hi[...], gn_lo[...], dot_nt)
        for a in range(2):
            for b in range(4):
                s = a * 4 + b
                west = h_w[par, b, :rows] if a == 0 else xv[0, b, :rows]
                beside = jnp.where(low, west, 0.0 if b == 0 else xv[a, b - 1, :rows])
                hi, lo = split(jnp.concatenate([xv[a, b, :rows], beside], axis=1))
                both = jnp.concatenate([hi, lo], axis=0)
                lhs[s, : 2 * rows] = both
                v2 = v2 + three(both, hi, g_hi[s], g_lo[s], dot_nt)
        coarse.start(jnp.concatenate(
            [jnp.where(low8, v2[16 * f : 16 * f + 8], v2[16 * f + 8 : 16 * f + 16]) for f in range(fields)], axis=0
        ))

        def local(s):
            wk[s, :rows] = three(lhs[s, : 2 * rows], lhs[s, :rows], s_hi[s], s_lo[s], dot)

        for s in (1, 2, 3, 5, 6, 7):
            local(s)
        hooks.get("inverse", nothing)()
        if groups:
            groups[2].start(total(groups[1]))
        each_of(copies, (1, 2, 3), receives, "wait_recv")
        for a in range(2):
            s = a * 4
            west = h_w[par, 0, :rows] if a == 0 else xv[0, 0, :rows]
            hi, lo = split(jnp.where(low, west, h_s[par, a, :rows]))
            lhs[s, :rows, 128:] = hi
            lhs[s, rows : 2 * rows, 128:] = lo
            local(s)
        hooks.get("upper", nothing)()
        above = [
            jnp.concatenate([
                h_n[par, a, :rows],
                jnp.where(low, h_nw[par, :rows] if a == 0 else h_n[par, 0, :rows], xv[a, 3, :rows]),
            ], axis=1)
            for a in range(2)
        ]
        hi, lo = split(jnp.concatenate(above, axis=0))
        both = three(jnp.concatenate([hi, lo], axis=0), hi, n_hi[...], n_lo[...], dot)
        upper = jnp.where(low, both[:rows], both[rows:])
        hooks.get("region", nothing)()
        coarse.wait()
        pieces = []
        for pair in range(gyn // 2):
            parts = []
            for f in range(fields):
                one, two = g1[par, 2 * pair, 8 * f : 8 * f + 8], g1[par, 2 * pair + 1, 8 * f : 8 * f + 8]
                parts.append(jnp.where(low8, one, pltpu.roll(two, 64, 1)))
                parts.append(jnp.where(low8, pltpu.roll(one, 64, 1), two))
            pieces.append(jnp.concatenate(parts, axis=0))
        hi, lo = split(jnp.concatenate(pieces, axis=1))
        back = three(jnp.concatenate([hi, lo], axis=0), hi, m_hi[...], m_lo[...], dot_nt)
        bhi, blo = split(back)
        bhl = jnp.concatenate([bhi, blo], axis=0)
        for s in range(8):
            full = wk[s, :rows] + three(bhl, bhi, g_hi[s], g_lo[s], dot)
            wk[s, :rows] = full
            if s < 4:
                wn[s, :rows] = full[:, 128:]
            if s == 3:
                each_of(copies, (4,), sends, "start")
        upper = upper + three(bhl, bhi, gn_hi[...], gn_lo[...], dot)
        summed = total(groups[2]) if groups else None
        each_of(copies, (4,), receives, "wait_recv")
        result = []
        for a in range(2):
            for b in range(4):
                s = a * 4 + b
                east = r_e[par, b, :rows] if a == 1 else wk[4 + b, :rows, 128:]
                if b < 3:
                    north = wk[s + 1, :rows, 128:]
                else:
                    north = pltpu.roll(upper, 64, 1) if a == 0 else upper
                got = wk[s, :rows, :128] + jnp.where(low, east, north)
                result.append(got * jnp.concatenate([keep[s]] * fields, axis=0))
        each_of(copies, (0, 1, 2, 3, 4), sends, "wait_send")
        for group in groups + (coarse,):
            group.finish()
        return jnp.stack(result), summed

    def residual_products():
        z = dv[...] * res[...]
        return [res[...] * z, z * wv[...], z * qv[...]]

    def step_of(line):
        rho = column(line, 0)
        beta = rho / sc[0]
        pq = column(line, 1) + beta * (2.0 * column(line, 2) + beta * sc[1])
        alpha = rho / pq
        sc[0] = rho
        sc[1] = pq
        return beta, alpha, dv[...] * res[...] + beta * pv[...]

    def advance(got, summed):
        beta, alpha, p = step_of(summed)
        pv[...] = p
        q = wv[...] + beta * qv[...]
        t = got + beta * tv[...]
        qv[...] = q
        tv[...] = t
        lam[...] += alpha * p
        res[...] -= alpha * q
        w = wv[...] - alpha * t
        wv[...] = w
        xv[:, :, :16] = (dv[...] * w).reshape(2, 4, 16, 128)
        return dots(residual_products())

    got, _ = apply(0, 2, None, {
        "corners": number_corners, "inverse": own_inverse, "upper": upper_block, "region": region_inverse,
    })
    slots.finish()
    for copy in early:
        pl.when(has_s)(lambda copy=copy: copy.wait_send())
    w, q = got[:, :16], got[:, 16:]
    wv[...] = w
    qv[...] = q
    xv[:, :, :16] = (dv[...] * w).reshape(2, 4, 16, 128)
    xv[:, :, 16:] = (dv[...] * q).reshape(2, 4, 16, 128)
    line = dots(residual_products() + [pv[...] * q])
    got, summed = apply(1, 2, line, {})
    tv[...] = got[:, 16:]
    sc[0] = column(small[8:9], 0)
    sc[1] = column(summed, 3)
    line = advance(got[:, :16], summed)

    def round_body(i, line):
        got, summed = apply(lax.rem(i, 2), 1, line, {})
        return advance(got, summed)

    line = lax.fori_loop(2, iters, round_body, line)

    last = stages(iters % 2)
    last[0].start(line)
    last[1].start(total(last[0]))
    last[2].start(total(last[1]))
    beta, alpha, p = step_of(total(last[2]))
    new_l = lam[...] + alpha * p
    new_r = res[...] - alpha * (wv[...] + beta * qv[...])
    for a in range(2):
        for b in range(4):
            s = a * 4 + b
            out_l[:, a, b, :] = new_l[s]
            out_r[:, a, b, :] = new_r[s]
            out_p[:, a, b, :] = p[s]
    for group in last:
        group.finish()


def shards(gxn, gyn, zn, yhn, duals, residual, direction, prev_rho, schur, coupling, ainv, emap, slot, active, scaling):
    yn = gxn // zn * yhn
    vmem = pl.BlockSpec(memory_space=pltpu.VMEM)
    field = jax.ShapeDtypeStruct(duals.shape, F32)
    tiles = lambda *lead: pltpu.VMEM(lead + (16, 128), F32)
    pair = lambda *lead: pltpu.VMEM(lead + (32, 128), F32)
    line = lambda *lead: pltpu.VMEM(lead + (1, 128), F32)
    dma = lambda *shape: pltpu.SemaphoreType.DMA(shape)
    return pl.pallas_call(
        functools.partial(kernel, gxn, gyn, zn, yhn, 6),
        out_shape=(field, field, field),
        in_specs=[vmem] * 11,
        out_specs=(vmem, vmem, vmem),
        scratch_shapes=[
            pltpu.VMEM((8, 256, 256), BF16), pltpu.VMEM((8, 256, 256), BF16),
            pltpu.VMEM((8, 128, 256), BF16), pltpu.VMEM((8, 128, 256), BF16),
            pltpu.VMEM((128, 64 * gyn), BF16), pltpu.VMEM((128, 64 * gyn), BF16),
            pltpu.VMEM((8, 64, 256), BF16),
            tiles(8), tiles(8), tiles(8), tiles(8), tiles(8), tiles(8), pair(2, 4), tiles(8), tiles(8),
            pltpu.VMEM((8, 32, 256), F32), pair(4),
            pair(2, 4), pair(2, 2), pair(2, 4), pair(2, 2), pair(2),
            pltpu.VMEM((2, gyn, 16, 128), F32), pltpu.VMEM((16, 128), F32),
            line(2, gyn // yhn), line(2, yn), line(2, zn), line(), line(), line(),
            line(gyn), line(), tiles(2),
            pltpu.VMEM((256, 128), F32), pltpu.VMEM((256, 128), F32), pltpu.VMEM((8, 128), F32), pltpu.VMEM((8, 128), F32),
            line(), line(),
            pltpu.VMEM((256, 128), BF16), pltpu.VMEM((256, 128), BF16), pltpu.VMEM((128, 128), BF16), pltpu.VMEM((128, 128), BF16),
            pltpu.VMEM((16, 128), F32),
            dma(5), dma(2, 5), dma(gyn), dma(2, gyn),
            dma(gyn // yhn), dma(2, gyn // yhn), dma(yn), dma(2, yn), dma(zn), dma(2, zn), dma(gyn), dma(gyn), dma(3), dma(3),
        ],
        compiler_params=pltpu.CompilerParams(collective_id=0, has_side_effects=True),
    )(duals, residual, direction, prev_rho.reshape(1, 16), schur.reshape(8, 256, 256), coupling.reshape(8, 8, 256), ainv[0], emap, slot, active, scaling)


def solution(mesh):
    gxn, gyn = mesh.shape["gx"], mesh.shape["gy"]
    zn = 8 if gxn % 8 == 0 else 2
    yhn = 2
    grid = P(None, "gx", "gy", None)
    cells = P("gx", "gy", None)
    return jax.shard_map(
        functools.partial(shards, gxn, gyn, zn, yhn),
        mesh=mesh,
        in_specs=(
            grid, grid, grid, P(), P("gx", "gy", None, None), P("gx", "gy", None, None), P("gx", None, None),
            cells, cells, cells, cells,
        ),
        out_specs=(grid, grid, grid),
        check_vma=False,
    )
```
